768 devices in a mesh: dp: 24 (over z, core), ctx: 32 (over x, y).
Axes of the slice: x: 4, y: 8, z: 12, core: 2. Of those that a mesh axis runs over, the one named last changes fastest.
Arguments:
- query_heads: bfloat16 [24, 4096, 1024], P('dp', 'ctx'), may hold values from -6 to 6
- key_heads: bfloat16 [24, 4096, 1024], P('dp', 'ctx'), may hold values from -6 to 6
- value_heads: bfloat16 [24, 4096, 1024], P('dp', 'ctx'), may hold values from -6 to 6
- grad_output: bfloat16 [24, 4096, 1024], P('dp', 'ctx'), may hold values from -6 to 6
- layer_input: bfloat16 [24, 4096, 1152], P('dp', 'ctx'), may hold values from -6 to 6
Outputs:
- grad_query: bfloat16 [24, 4096, 1024], P('dp', 'ctx')
- grad_key: bfloat16 [24, 4096, 1024], P('dp', 'ctx')
- grad_value: bfloat16 [24, 4096, 1024], P('dp', 'ctx')
- grad_weight: float32 [1152, 1024], P('dp', 'ctx')
The draws below stay inside these ranges and needn't reach their ends.
All inputs are finite; a program needn't handle non-finite values.
Results may differ from the reference program's by a relative error of at most 0.008.
Values sent between devices are 32-bit elements; how exact they have to be, the bound alone decides.
No kernel may reach another device: no remote copies, remote signals or barrier semaphores. Data moves between devices by JAX's collectives and lax.ppermute only.
A program may use at most 128 MiB of HBM per device.

```python
import math
import jax
import jax.numpy as jnp
from jax import lax

HD = 128
HV = 8
DW = 1152
TOK_DEV = 128
VW = 1024
SEQ = 4096
BATCH = 24
N_DP = 24


def block_levels(rng, dims, cuts, smallest, high):
    loudness, own = 1.0, jax.random.fold_in(rng, 6)
    for axis_at, shards_of in cuts:
        heights = jnp.exp(jax.random.uniform(jax.random.fold_in(own, axis_at), (shards_of,), jnp.float32, smallest / len(cuts), high / len(cuts)))
        loudness = loudness * jnp.repeat(heights, dims[axis_at] // shards_of).reshape([-1 if axis == axis_at else 1 for axis in range(len(dims))])
    return loudness


def normal_values(rng, extent, scale, most, pieces=(), held_as=jnp.bfloat16):
    level = block_levels(rng, extent, pieces, -0.22, 0.18) if pieces else 1.0
    values = jax.random.normal(rng, extent, jnp.float32) * scale * level
    return jnp.minimum(jnp.maximum(values, -most), most).astype(held_as)


def setup_inputs(seed: int = 0) -> dict:
    streams_of = jax.random.split(jax.random.key(seed), 6)
    query_heads = normal_values(streams_of[0], (BATCH, SEQ, VW), 1.0, 6.0, ((0, 24), (1, 32)))
    key_heads = normal_values(streams_of[1], (BATCH, SEQ, VW), 1.0, 6.0, ((0, 24), (1, 32)))
    value_heads = normal_values(streams_of[2], (BATCH, SEQ, VW), 1.0, 6.0, ((0, 24), (1, 32)))
    grad_output = normal_values(streams_of[3], (BATCH, SEQ, VW), 1.0, 6.0, ((0, 24), (1, 32)))
    layer_input = normal_values(streams_of[4], (BATCH, SEQ, DW), 1.0, 6.0, ((0, 24), (1, 32)))
    return {"query_heads": query_heads, "key_heads": key_heads, "value_heads": value_heads, "grad_output": grad_output, "layer_input": layer_input}


def reference(query_heads, key_heads, value_heads, grad_output, layer_input):
    length = query_heads.shape[1]
    blocks = length // TOK_DEV
    scale = 1.0 / math.sqrt(HD * length)
    rscale = 1.0 / math.sqrt(N_DP * length)
    highest = lax.Precision.HIGHEST
    rows = jnp.arange(TOK_DEV)
    causal = (rows[:, None] >= rows[None, :]).astype(jnp.float32)

    def split(array):
        return array.reshape(blocks, TOK_DEV, HV, HD).astype(jnp.float32)

    def one(total, items):
        query, keyed, valued, cotan, inputs = items
        qf, kf, vf, gf = (split(query), split(keyed), split(valued), split(cotan))
        kv_block = jnp.einsum('bthi,bthj->bhij', kf, vf, precision=highest)
        qg_block = jnp.einsum('bthi,bthj->bhij', qf, gf, precision=highest)
        zero = jnp.zeros((1, HV, HD, HD), jnp.float32)
        prefix = jnp.concatenate([zero, jnp.cumsum(kv_block, 0)[:-1]], 0)
        suffix = jnp.concatenate([jnp.cumsum(qg_block[::-1], 0)[:-1][::-1], zero], 0)
        score_raw = jnp.einsum('bthd,bshd->bhts', qf, kf, precision=highest)
        grad_raw = jnp.einsum('bthd,bshd->bhts', gf, vf, precision=highest)
        score_w = (scale * score_raw * causal).astype(jnp.bfloat16).astype(jnp.float32)
        grad_w = (scale * grad_raw * causal).astype(jnp.bfloat16).astype(jnp.float32)
        dquery = jnp.einsum('bhts,bshd->bthd', grad_w, kf, precision=highest)
        dquery = dquery + scale * jnp.einsum('bthj,bhij->bthi', gf, prefix, precision=highest)
        dkey = jnp.einsum('bhts,bthd->bshd', grad_w, qf, precision=highest)
        dkey = dkey + scale * jnp.einsum('bshj,bhij->bshi', vf, suffix, precision=highest)
        dvalue = jnp.einsum('bhts,bthd->bshd', score_w, gf, precision=highest)
        dvalue = dvalue + scale * jnp.einsum('bshi,bhij->bshj', kf, suffix, precision=highest)
        dquery = dquery.reshape(length, HV * HD).astype(jnp.bfloat16)
        dkey = dkey.reshape(length, HV * HD).astype(jnp.bfloat16)
        dvalue = dvalue.reshape(length, HV * HD).astype(jnp.bfloat16)
        total = total + jnp.dot(inputs.T, dvalue, preferred_element_type=jnp.float32)
        return (total, (dquery, dkey, dvalue))
    start = jnp.zeros((layer_input.shape[2], query_heads.shape[2]), jnp.float32)
    total, grads = lax.scan(one, start, (query_heads, key_heads, value_heads, grad_output, layer_input))
    return (grads[0], grads[1], grads[2], total * rscale)
```

```python
import math

import jax
import jax.numpy as jnp
import numpy as np
from jax import lax
from jax.experimental import pallas as pl
from jax.experimental.pallas import tpu as pltpu
from jax.sharding import Mesh
from jax.sharding import PartitionSpec as P

HD = 128
HV = 8
DW = 1152
TOK = 128
VW = HV * HD
BF = jnp.bfloat16
F32 = jnp.float32
INTERPRET = False


def dot(a, b, ca, cb):
    if INTERPRET:
        a, b = a.astype(F32), b.astype(F32)
    return lax.dot_general(a, b, (((ca,), (cb,)), ((), ())), preferred_element_type=F32)


def call(body, outs, *args, name):
    return pl.pallas_call(
        body,
        out_shape=outs,
        name=name,
        interpret=INTERPRET,
    )(*args)


def head(h):
    return slice(h * HD, (h + 1) * HD)


def states_body(q_ref, k_ref, v_ref, g_ref, st_ref):
    rows = st_ref.shape[2]
    for h in range(HV):
        s = head(h)
        for which, (a_ref, b_ref) in enumerate(((k_ref, v_ref), (q_ref, g_ref))):
            block = dot(a_ref[:, s], b_ref[:, s], 0, 0)
            if rows <= HD:
                per = HD // rows
                st_ref[h * per : (h + 1) * per, which] = block.reshape(per, rows, HD)
            else:
                at = h * HD
                st_ref[at // rows, which, at % rows : at % rows + HD] = block


def intra_body(scale, q_ref, k_ref, v_ref, g_ref, dq_ref, dk_ref, dv_ref):
    t = lax.broadcasted_iota(jnp.int32, (TOK, TOK), 0)
    u = lax.broadcasted_iota(jnp.int32, (TOK, TOK), 1)
    causal = t >= u
    for h in range(HV):
        s = head(h)
        q, k, v, g = q_ref[:, s], k_ref[:, s], v_ref[:, s], g_ref[:, s]
        score_w = jnp.where(causal, scale * dot(q, k, 1, 1), 0.0).astype(BF)
        grad_w = jnp.where(causal, scale * dot(g, v, 1, 1), 0.0).astype(BF)
        dq_ref[:, s] = dot(grad_w, k, 1, 0)
        dk_ref[:, s] = dot(grad_w, q, 0, 0)
        dv_ref[:, s] = dot(score_w, g, 0, 0)


def scan_body(in_ref, out_ref):
    n = in_ref.shape[0]
    total = jnp.zeros(in_ref.shape[2:], F32)
    for i in range(n):
        out_ref[i, 0] = total
        if i < n - 1:
            total = total + in_ref[i, 0]
    total = jnp.zeros(in_ref.shape[2:], F32)
    for i in reversed(range(n)):
        out_ref[i, 1] = total
        if i > 0:
            total = total + in_ref[i, 1]


def final_body(scale, nx, k_ref, v_ref, g_ref, dqi_ref, dki_ref, dvi_ref, st_ref, perm_ref, dq_ref, dk_ref, dv_ref, send_ref):
    rows = st_ref.shape[2]
    wide = VW // nx

    def state(h, which):
        if rows <= HD:
            per = HD // rows
            block = st_ref[h * per : (h + 1) * per, which].reshape(HD, HD)
        else:
            at = h * HD
            block = st_ref[at // rows, which, at % rows : at % rows + HD]
        return block.astype(BF)

    for h in range(HV):
        s = head(h)
        suffix = state(h, 1)
        dv_ref[:, s] = (dvi_ref[:, s] + scale * dot(k_ref[:, s], suffix, 1, 0)).astype(BF)
        dk_ref[:, s] = (dki_ref[:, s] + scale * dot(v_ref[:, s], suffix, 1, 1)).astype(BF)
        dq_ref[:, s] = (dqi_ref[:, s] + scale * dot(g_ref[:, s], state(h, 0), 1, 1)).astype(BF)
    for b in range(nx):
        moved = dot(dv_ref[:, b * wide : (b + 1) * wide], perm_ref[...], 1, 0)
        send_ref[2 * b] = moved[:, : wide // 2]
        send_ref[2 * b + 1] = moved[:, wide // 2 :]


def pack_body(place_ref, mine_ref, other_ref, out_ref):
    nx = mine_ref.shape[0]
    for d in range(nx):
        slot = 2 * lax.rem(place_ref[0] + nx - d, nx)
        out_ref[slot + place_ref[1]] = mine_ref[d].astype(BF)
        out_ref[slot + 1 - place_ref[1]] = other_ref[d].astype(BF)


def weight_body(rscale, dv_ref, x_ref, out_ref):
    n = dv_ref.shape[0]
    total = None
    for i in range(n):
        part = dot(dv_ref[i].astype(BF), x_ref[i], 0, 0)
        total = part if total is None else total + part
    out_ref[...] = total * rscale


def fold_body(in_ref, out_ref):
    total = in_ref[0]
    for i in range(1, in_ref.shape[0]):
        total = total + in_ref[i]
    n, half, wide = out_ref.shape
    rows = wide // 2
    for i in range(n):
        part = total[:, i * rows : (i + 1) * rows]
        out_ref[i] = jnp.concatenate([part[:half], part[half:]], axis=1)


def last_body(in_ref, out_ref):
    n, half, wide = in_ref.shape
    rows = wide // 2
    pieces = []
    for c in range(2):
        total = in_ref[c]
        for z in range(1, n // 2):
            total = total + in_ref[2 * z + c]
        pieces += [total[:, :rows], total[:, rows:]]
    out_ref[...] = jnp.concatenate(pieces, axis=0).T


def column_order(nx, ny):
    wide = VW // nx
    width = wide // ny
    perm = np.zeros((wide, wide), np.float32)
    for to in range(wide):
        c, rest = divmod(to, wide // 2)
        y, j = divmod(rest, width // 2)
        perm[y * width + c * (width // 2) + j, to] = 1.0
    return perm


def on_device(sizes, query_heads, key_heads, value_heads, grad_output, layer_input):
    nz, nx, ny = sizes
    nc = nx * ny
    length = TOK * nc
    scale = 1.0 / math.sqrt(HD * length)
    rscale = 1.0 / math.sqrt(2 * nz * length)
    q, k, v, g = query_heads[0], key_heads[0], value_heads[0], grad_output[0]
    rows = VW // nc

    def shaped(*shape, dtype=F32):
        return jax.ShapeDtypeStruct(shape, dtype)

    own = layer_input[0].astype(F32)
    shifted = [own]
    for d in range(1, nx):
        shifted.append(lax.ppermute(own, "x", [(i, (i + d) % nx) for i in range(nx)]))
    mine = jnp.stack(shifted)
    other = lax.ppermute(mine, "c", [(0, 1), (1, 0)])
    place = jnp.stack([lax.axis_index("x"), lax.axis_index("c")]).astype(jnp.int32)
    inputs = pl.pallas_call(
        pack_body,
        in_specs=[pl.BlockSpec(memory_space=pltpu.SMEM)] + [pl.BlockSpec(memory_space=pltpu.VMEM)] * 2,
        out_shape=shaped(2 * nx, TOK, DW, dtype=BF),
        name="pack",
        interpret=INTERPRET,
    )(place, mine, other)

    states = call(states_body, shaped(nc, 2, rows, HD), q, k, v, g, name="states")
    held = lax.all_to_all(states, ("x", "y"), 0, 0, tiled=True)
    intra = call(
        lambda *refs: intra_body(scale, *refs), [shaped(TOK, VW)] * 3, q, k, v, g, name="intra"
    )
    entering = call(scan_body, shaped(nc, 2, rows, HD), held, name="scan")
    state = lax.all_to_all(entering, ("x", "y"), 0, 0, tiled=True)
    perm = jnp.asarray(column_order(nx, ny), BF)
    wide = VW // nx
    dq, dk, dv, send = call(
        lambda *refs: final_body(scale, nx, *refs),
        [shaped(TOK, VW, dtype=BF)] * 3 + [shaped(2 * nx, TOK, wide // 2)],
        k, v, g, *intra, state, perm, name="final",
    )
    columns = lax.all_to_all(send, ("x", "c"), 0, 0, tiled=True)
    term = call(
        lambda *refs: weight_body(rscale, *refs), shaped(wide // 2, DW), columns, inputs, name="weight"
    )
    half = wide // 2 // ny
    terms = lax.all_to_all(term.reshape(ny, half, DW), "y", 0, 0, tiled=True)
    out_rows = DW // (2 * nz)
    folded = call(fold_body, shaped(2 * nz, half // 2, 2 * out_rows), terms, name="fold")
    parts = lax.all_to_all(folded, ("z", "c"), 0, 0, tiled=True)
    weight = call(last_body, shaped(out_rows, 2 * half), parts, name="last")
    return dq[None], dk[None], dv[None], weight


def solution(mesh):
    nz, nx, ny = mesh.shape["dp"] // 2, SHAPE_X, mesh.shape["ctx"] // SHAPE_X
    inner = Mesh(mesh.devices.reshape(nz, 2, nx, ny), ("z", "c", "x", "y"))
    spec = P(("z", "c"), ("x", "y"), None)
    return jax.shard_map(
        lambda *arrays: on_device((nz, nx, ny), *arrays),
        mesh=inner,
        in_specs=(spec,) * 5,
        out_specs=(spec, spec, spec, P(("z", "c"), ("x", "y"))),
        check_vma=False,
    )


SHAPE_X = 4
```

```python
import math

import jax
import jax.numpy as jnp
from jax import lax
from jax.experimental import pallas as pl
from jax.experimental.pallas import tpu as pltpu
from jax.sharding import Mesh
from jax.sharding import PartitionSpec as P

HD = 128
HV = 8
DW = 1152
TOK = 128
VW = HV * HD
BF = jnp.bfloat16
F32 = jnp.float32
INTERPRET = False


def dot(a, b, ca, cb):
    if INTERPRET:
        a, b = a.astype(F32), b.astype(F32)
    return lax.dot_general(a, b, (((ca,), (cb,)), ((), ())), preferred_element_type=F32)


def call(body, outs, *args):
    return pl.pallas_call(body, out_shape=outs, interpret=INTERPRET)(*args)


def head(h):
    return slice(h * HD, (h + 1) * HD)


def states_body(q_ref, k_ref, v_ref, g_ref, st_ref):
    rows = st_ref.shape[2]
    for h in range(HV):
        s = head(h)
        for which, (a_ref, b_ref) in enumerate(((k_ref, v_ref), (q_ref, g_ref))):
            block = dot(a_ref[:, s], b_ref[:, s], 0, 0)
            if rows <= HD:
                per = HD // rows
                st_ref[h * per : (h + 1) * per, which] = block.reshape(per, rows, HD)
            else:
                st_ref[h * HD // rows, which, h * HD % rows : h * HD % rows + HD] = block


def load_state(st_ref, which, h):
    rows = st_ref.shape[2]
    if rows <= HD:
        per = HD // rows
        block = st_ref[h * per : (h + 1) * per, which].reshape(HD, HD)
    else:
        block = st_ref[h * HD // rows, which, h * HD % rows : h * HD % rows + HD]
    return block.astype(BF)


def intra_body(scale, q_ref, k_ref, v_ref, g_ref, dq_ref, dk_ref, dv_ref):
    t = lax.broadcasted_iota(jnp.int32, (TOK, TOK), 0)
    u = lax.broadcasted_iota(jnp.int32, (TOK, TOK), 1)
    causal = t >= u
    for h in range(HV):
        s = head(h)
        q, k, v, g = q_ref[:, s], k_ref[:, s], v_ref[:, s], g_ref[:, s]
        score_w = jnp.where(causal, scale * dot(q, k, 1, 1), 0.0).astype(BF)
        grad_w = jnp.where(causal, scale * dot(g, v, 1, 1), 0.0).astype(BF)
        dq_ref[:, s] = dot(grad_w, k, 1, 0)
        dk_ref[:, s] = dot(grad_w, q, 0, 0)
        dv_ref[:, s] = dot(score_w, g, 0, 0)


def scan_body(in_ref, out_ref):
    n = in_ref.shape[0]
    for which, order in enumerate((range(n), range(n)[::-1])):
        total = jnp.zeros(in_ref.shape[2:], F32)
        for i in order:
            out_ref[i, which] = total
            total = total + in_ref[i, which]


def value_body(scale, k_ref, dvi_ref, st_ref, perm_ref, dv_ref, send_ref):
    for h in range(HV):
        s = head(h)
        inter = dot(k_ref[:, s], load_state(st_ref, 1, h), 1, 0)
        dv_ref[:, s] = (dvi_ref[:, s] + scale * inter).astype(BF)
    moved = dot(dv_ref[...], perm_ref[...], 1, 0)
    wide = send_ref.shape[2]
    for m in range(send_ref.shape[0]):
        send_ref[m] = moved[:, m * wide : (m + 1) * wide]


def outer_body(scale, g_ref, v_ref, dqi_ref, dki_ref, st_ref, dq_ref, dk_ref):
    for h in range(HV):
        s = head(h)
        inter = dot(g_ref[:, s], load_state(st_ref, 0, h), 1, 1)
        dq_ref[:, s] = (dqi_ref[:, s] + scale * inter).astype(BF)
        inter = dot(v_ref[:, s], load_state(st_ref, 1, h), 1, 1)
        dk_ref[:, s] = (dki_ref[:, s] + scale * inter).astype(BF)


def pack_body(*refs):
    for i, ref in enumerate(refs[:-1]):
        refs[-1][i] = ref[...].astype(BF)


def weight_body(rscale, place_ref, dv_ref, x_ref, out_ref):
    n = dv_ref.shape[0] // 2
    total = None
    for i in range(2 * n):
        slot = 2 * lax.rem(place_ref[0] + n - i // 2, n) + lax.rem(place_ref[1] + i % 2, 2)
        part = dot(dv_ref[slot].astype(BF), x_ref[i], 0, 0)
        total = part if total is None else total + part
    total = total * rscale
    blocks, cols, _ = out_ref.shape
    for i in range(blocks):
        out_ref[i] = total[i * cols : (i + 1) * cols]


def fold_body(in_ref, out_ref):
    total = in_ref[0]
    for i in range(1, in_ref.shape[0]):
        total = total + in_ref[i]
    n = out_ref.shape[0]
    cols, rows = total.shape[0], total.shape[1] // n
    for i in range(n):
        part = total[:, i * rows : (i + 1) * rows]
        out_ref[i] = jnp.concatenate([part[j : j + 1] for j in range(cols)], axis=1)


def last_body(members, in_ref, out_ref):
    rows = out_ref.shape[1]
    cols = in_ref.shape[2] // rows
    for m in range(members):
        total = in_ref[m]
        for i in range(m + members, in_ref.shape[0], members):
            total = total + in_ref[i]
        for j in range(cols):
            at = m * cols + j
            out_ref[at : at + 1] = total[:, j * rows : (j + 1) * rows]


def on_device(sizes, query_heads, key_heads, value_heads, grad_output, layer_input):
    na, nb, nx, ny = sizes
    nc = nx * ny
    members = 2 * nb
    length = TOK * nc
    scale = 1.0 / math.sqrt(HD * length)
    rscale = 1.0 / math.sqrt(2 * na * nb * length)
    q, k, v, g = query_heads[0], key_heads[0], value_heads[0], grad_output[0]
    rows = VW // nc
    wide = VW // members
    cols = wide // nc

    def shaped(*shape, dtype=F32):
        return jax.ShapeDtypeStruct(shape, dtype)

    states = shaped(nc, 2, rows, HD)
    flat = shaped(TOK, VW)
    flat_bf = shaped(TOK, VW, dtype=BF)

    def exchange(array, axes):
        return lax.all_to_all(array, axes, 0, 0, tiled=True)

    held = exchange(call(states_body, states, q, k, v, g), ("x", "y"))

    own = layer_input[0].astype(F32)
    swap = [(0, 1), (1, 0)]
    both = [own, lax.ppermute(own, "c", swap)]
    for d in range(1, nb):
        array = lax.ppermute(own, "b", [(i, (i + d) % nb) for i in range(nb)])
        both += [array, lax.ppermute(array, "c", swap)]
    inputs = call(pack_body, shaped(members, TOK, DW, dtype=BF), *both)
    place = jnp.stack([lax.axis_index("b"), lax.axis_index("c")]).astype(jnp.int32)

    dqi, dki, dvi = call(lambda *refs: intra_body(scale, *refs), [flat] * 3, q, k, v, g)
    at = jnp.arange(VW)
    block, rest = jnp.divmod(at, VW // nc)
    member, j = jnp.divmod(rest, cols)
    perm = (at[None, :] == (member * wide + block * cols + j)[:, None]).astype(BF)

    state = exchange(call(scan_body, states, held), ("x", "y"))
    dv, send = call(
        lambda *refs: value_body(scale, *refs),
        [flat_bf, shaped(members, TOK, wide)],
        k, dvi, state, perm,
    )
    columns = exchange(send, ("b", "c"))
    dq, dk = call(lambda *refs: outer_body(scale, *refs), [flat_bf] * 2, g, v, dqi, dki, state)
    term = pl.pallas_call(
        lambda *refs: weight_body(rscale, *refs),
        in_specs=[pl.BlockSpec(memory_space=pltpu.SMEM)] + [pl.BlockSpec(memory_space=pltpu.VMEM)] * 2,
        out_shape=shaped(nc, cols, DW),
        name="weight",
        interpret=INTERPRET,
    )(place, columns, inputs)
    terms = exchange(term, ("x", "y"))
    out_rows = DW // (members * na)
    folded = call(fold_body, shaped(members * na, 1, cols * out_rows), terms)
    parts = exchange(folded, ("a", "b", "c"))
    weight = call(lambda *refs: last_body(members, *refs), shaped(members * cols, out_rows), parts)
    return dq[None], dk[None], dv[None], weight.T


def solution(mesh):
    nx, nb = SPLIT
    sizes = (mesh.shape["dp"] // 2 // nb, nb, nx, mesh.shape["ctx"] // nx)
    na, nb, nx, ny = sizes
    inner = Mesh(mesh.devices.reshape(na, nb, 2, nx, ny), ("a", "b", "c", "x", "y"))
    spec = P(("a", "b", "c"), ("x", "y"), None)

    def body(*arrays):
        return on_device(sizes, *arrays)

    return jax.shard_map(
        body,
        mesh=inner,
        in_specs=(spec,) * 5,
        out_specs=(spec, spec, spec, P(("a", "b", "c"), ("x", "y"))),
        check_vma=False,
    )


SPLIT = (4, 4)
```

```python
import math

import jax
import jax.numpy as jnp
from jax import lax
from jax.experimental import pallas as pl
from jax.experimental.pallas import tpu as pltpu
from jax.sharding import Mesh
from jax.sharding import PartitionSpec as P

HD = 128
HV = 8
DW = 1152
TOK = 128
VW = HV * HD
BF = jnp.bfloat16
F32 = jnp.float32
INTERPRET = False


def dot(a, b, ca, cb):
    if INTERPRET:
        a, b = a.astype(F32), b.astype(F32)
    return lax.dot_general(a, b, (((ca,), (cb,)), ((), ())), preferred_element_type=F32)


def call(body, outs, *args):
    return pl.pallas_call(body, out_shape=outs, interpret=INTERPRET)(*args)


def head(h):
    return slice(h * HD, (h + 1) * HD)


def states_body(q_ref, k_ref, v_ref, g_ref, st_ref):
    rows = st_ref.shape[1] // 2
    for h in range(HV):
        s = head(h)
        for which, (a_ref, b_ref) in enumerate(((k_ref, v_ref), (q_ref, g_ref))):
            block = dot(a_ref[:, s], b_ref[:, s], 0, 0)
            at = which * rows
            if rows <= HD:
                per = HD // rows
                st_ref[h * per : (h + 1) * per, at : at + rows] = block.reshape(per, rows, HD)
            else:
                at += h * HD % rows
                st_ref[h * HD // rows, at : at + HD] = block


def load_state(st_ref, which, h):
    rows = st_ref.shape[1] // 2
    at = which * rows
    if rows <= HD:
        per = HD // rows
        block = st_ref[h * per : (h + 1) * per, at : at + rows].reshape(HD, HD)
    else:
        at += h * HD % rows
        block = st_ref[h * HD // rows, at : at + HD]
    return block.astype(BF)


def intra_body(scale, q_ref, k_ref, v_ref, g_ref, dq_ref, dk_ref, dv_ref):
    t = lax.broadcasted_iota(jnp.int32, (TOK, TOK), 0)
    u = lax.broadcasted_iota(jnp.int32, (TOK, TOK), 1)
    causal = t >= u
    for h in range(HV):
        s = head(h)
        q, k, v, g = q_ref[:, s], k_ref[:, s], v_ref[:, s], g_ref[:, s]
        score_w = jnp.where(causal, scale * dot(q, k, 1, 1), 0.0).astype(BF)
        grad_w = jnp.where(causal, scale * dot(g, v, 1, 1), 0.0).astype(BF)
        dq_ref[:, s] = dot(grad_w, k, 1, 0)
        dk_ref[:, s] = dot(grad_w, q, 0, 0)
        dv_ref[:, s] = dot(score_w, g, 0, 0)


def scan_body(in_ref, out_ref):
    n, rows = in_ref.shape[0], in_ref.shape[1] // 2
    for which, order in enumerate((range(n), range(n)[::-1])):
        part = slice(which * rows, (which + 1) * rows)
        total = jnp.zeros((rows, HD), F32)
        for i in order:
            out_ref[i, part] = total
            total = total + in_ref[i, part]


def value_body(scale, k_ref, dvi_ref, st_ref, perm_ref, dv_ref, send_ref):
    for h in range(HV):
        s = head(h)
        inter = dot(k_ref[:, s], load_state(st_ref, 1, h), 1, 0)
        dv_ref[:, s] = (dvi_ref[:, s] + scale * inter).astype(BF)
    wide = perm_ref.shape[0]
    for b in range(VW // wide):
        moved = dot(dv_ref[:, b * wide : (b + 1) * wide], perm_ref[...], 1, 0)
        send_ref[2 * b] = moved[:, : wide // 2]
        send_ref[2 * b + 1] = moved[:, wide // 2 :]


def outer_body(scale, g_ref, v_ref, dqi_ref, dki_ref, st_ref, dq_ref, dk_ref):
    for h in range(HV):
        s = head(h)
        inter = dot(g_ref[:, s], load_state(st_ref, 0, h), 1, 1)
        dq_ref[:, s] = (dqi_ref[:, s] + scale * inter).astype(BF)
        inter = dot(v_ref[:, s], load_state(st_ref, 1, h), 1, 1)
        dk_ref[:, s] = (dki_ref[:, s] + scale * inter).astype(BF)


def pack_body(*refs):
    for i, ref in enumerate(refs[:-1]):
        refs[-1][i] = ref[...].astype(BF)


def weight_body(rscale, place_ref, dv_ref, x_ref, out_ref):
    n = dv_ref.shape[0] // 2
    columns = []
    for i in range(2 * n):
        slot = 2 * lax.rem(place_ref[0] + n - i // 2, n) + lax.rem(place_ref[1] + i % 2, 2)
        columns.append(dv_ref[slot].astype(BF))
    tokens = x_ref[...].reshape(2 * n * TOK, DW)
    out_ref[...] = dot(jnp.concatenate(columns, axis=0), tokens, 0, 0) * rscale


def fold_body(in_ref, out_ref):
    total = in_ref[0]
    for i in range(1, in_ref.shape[0]):
        total = total + in_ref[i]
    n, half, wide = out_ref.shape
    rows = wide // 2
    for i in range(n):
        part = total[:, i * rows : (i + 1) * rows]
        out_ref[i] = jnp.concatenate([part[:half], part[half:]], axis=1)


def last_body(in_ref, out_ref):
    n, half, wide = in_ref.shape
    rows = wide // 2
    for c in range(2):
        total = in_ref[c]
        for z in range(1, n // 2):
            total = total + in_ref[2 * z + c]
        at = 2 * c * half
        out_ref[at : at + half] = total[:, :rows]
        out_ref[at + half : at + 2 * half] = total[:, rows:]


def on_device(sizes, query_heads, key_heads, value_heads, grad_output, layer_input):
    nz, nx, ny = sizes
    nc = nx * ny
    length = TOK * nc
    scale = 1.0 / math.sqrt(HD * length)
    rscale = 1.0 / math.sqrt(2 * nz * length)
    q, k, v, g = query_heads[0], key_heads[0], value_heads[0], grad_output[0]
    wide = VW // nx
    width = wide // ny
    half = width // 2

    def shaped(*shape, dtype=F32):
        return jax.ShapeDtypeStruct(shape, dtype)

    states = shaped(nc, 2 * VW // nc, HD)
    flat = shaped(TOK, VW)
    flat_bf = shaped(TOK, VW, dtype=BF)

    def exchange(array, axes):
        return lax.all_to_all(array, axes, 0, 0, tiled=True)

    held = exchange(call(states_body, states, q, k, v, g), ("x", "y"))

    own = layer_input[0].astype(F32)
    swap = [(0, 1), (1, 0)]
    both = [own, lax.ppermute(own, "c", swap)]
    for d in range(1, nx):
        array = lax.ppermute(own, "x", [(i, (i + d) % nx) for i in range(nx)])
        both += [array, lax.ppermute(array, "c", swap)]
    inputs = call(pack_body, shaped(2 * nx, TOK, DW, dtype=BF), *both)
    place = jnp.stack([lax.axis_index("x"), lax.axis_index("c")]).astype(jnp.int32)

    dqi, dki, dvi = call(lambda *refs: intra_body(scale, *refs), [flat] * 3, q, k, v, g)
    at = jnp.arange(wide)
    to = at % width // half * (wide // 2) + at // width * half + at % half
    perm = (at[None, :] == to[:, None]).astype(BF)

    state = exchange(call(scan_body, states, held), ("x", "y"))
    dv, send = call(
        lambda *refs: value_body(scale, *refs),
        [flat_bf, shaped(2 * nx, TOK, wide // 2)],
        k, dvi, state, perm,
    )
    columns = exchange(send, ("x", "c"))
    dq, dk = call(lambda *refs: outer_body(scale, *refs), [flat_bf] * 2, g, v, dqi, dki, state)
    term = pl.pallas_call(
        lambda *refs: weight_body(rscale, *refs),
        in_specs=[pl.BlockSpec(memory_space=pltpu.SMEM)] + [pl.BlockSpec(memory_space=pltpu.VMEM)] * 2,
        out_shape=shaped(wide // 2, DW),
        name="weight",
        interpret=INTERPRET,
    )(place, columns, inputs)
    terms = exchange(term.reshape(ny, half, DW), "y")
    rows = DW // (2 * nz)
    folded = call(fold_body, shaped(2 * nz, half // 2, 2 * rows), terms)
    parts = exchange(folded, ("z", "c"))
    weight = call(last_body, shaped(width, rows), parts)
    return dq[None], dk[None], dv[None], weight.T


def solution(mesh):
    nx = SHAPE_X
    sizes = (mesh.shape["dp"] // 2, nx, mesh.shape["ctx"] // nx)
    inner = Mesh(mesh.devices.reshape(sizes[0], 2, *sizes[1:]), ("z", "c", "x", "y"))
    spec = P(("z", "c"), ("x", "y"), None)

    def body(*arrays):
        return on_device(sizes, *arrays)

    return jax.shard_map(
        body,
        mesh=inner,
        in_specs=(spec,) * 5,
        out_specs=(spec, spec, spec, P(("z", "c"), ("x", "y"))),
        check_vma=False,
    )


SHAPE_X = 4
```
